128 devices in a mesh: row: 16 (over x, z_lo, core), col: 4 (over y), win: 2 (over z_hi).
Axes of the slice: x: 4, y: 4, z: 4 (z_hi: 2, z_lo: 2; z = z_hi * 2 + z_lo), core: 2. Of those that a mesh axis runs over, the one named last changes fastest.
Arguments:
- spectra: float32 [2, 2, 64, 2, 16384], P('win', None, ('row', 'col')), may hold values from -8 to 8
- tile_rows: int32 [8256], P(('row', 'col')), may hold values from 0 to 127, as said below
- tile_cols: int32 [8256], P(('row', 'col')), may hold values from 0 to 127, as said below
Outputs:
- cross: float32 [8256, 2, 2, 128, 128], P(('row', 'col'), None, None, 'win')
The draws below stay inside these ranges and needn't reach their ends.
Inputs may be any that keep to these rules, and one draw needn't show every extreme that they name: tile_rows[k] <= tile_cols[k] for every k, and the pairs (tile_rows[k], tile_cols[k]) are all pairs of channel blocks with row block at most column block, each exactly once, in an order drawn from the seed. `tile_cols`: see tile_rows.
All inputs are finite; a program needn't handle non-finite values.
Results may differ from the reference program's by a relative error of at most 0.006.
Values may be sent and summed in bfloat16 or wider, within the bound.
A program may use at most 128 MiB of HBM per device.

```python
import jax
import jax.numpy as jnp
from jax import lax

CHANNELS = 16384
BLOCK = 128
FREQS = 2
BLOCKS = 128
GROUPS = 2
WIN_GROUP = 64
WINDOWS = 128
PAIR_TILES = 8256
TILES_DEV = 129


def tile_pairs(key):
    first, second = jnp.triu_indices(BLOCKS)
    shuffle = jax.random.permutation(jax.random.fold_in(key, 7), first.shape[0])
    return (first[shuffle].astype(jnp.int32), second[shuffle].astype(jnp.int32))


def draw_tile_rows(key, part):
    return tile_pairs(key)[0]


def draw_tile_cols(key, part):
    return tile_pairs(key)[1]


def levels(key, extent, pieces, low, high):
    def one(axis_at, blocks):
        draws = jax.random.uniform(jax.random.fold_in(jax.random.fold_in(key, 6), axis_at), (blocks,), jnp.float32, low / len(pieces), high / len(pieces))
        return jnp.repeat(jnp.exp(draws), extent[axis_at] // blocks).reshape((-1,) + (1,) * (len(extent) - axis_at - 1))

    factor_of = one(*pieces[0])
    for cut in pieces[1:]:
        factor_of = factor_of * one(*cut)
    return factor_of


def centred(stream_key, shape, scale, limit, cuts=(), kind=jnp.bfloat16):
    values = jax.random.normal(stream_key, shape, jnp.float32) * scale
    if len(cuts) > 0:
        values = levels(stream_key, shape, cuts, -0.22, 0.18) * values
    return jnp.clip(values, min=-limit, max=limit).astype(kind)


def setup_inputs(seed: int = 0) -> dict:
    streams_of = jax.random.split(jax.random.key(seed), 4)
    return {
        "spectra": centred(streams_of[0], (GROUPS, FREQS, WIN_GROUP, 2, CHANNELS), 1.5, 8.0, ((0, 2), (2, 64)), jnp.float32),
        "tile_rows": draw_tile_rows(jax.random.fold_in(streams_of[3], 71), 0),
        "tile_cols": draw_tile_cols(jax.random.fold_in(streams_of[3], 71), 0),
    }


def whiten(spectra):
    power_sum = lax.optimization_barrier(jnp.sum(spectra * spectra, axis=(1, 3), keepdims=True)) / spectra.shape[1]
    return (spectra / jnp.maximum(jnp.sqrt(power_sum), 1.0)).astype(jnp.bfloat16)

def reference(spectra, tile_rows, tile_cols):
    whitened = whiten(spectra).astype(jnp.float32)
    blocks = whitened.reshape(GROUPS, FREQS, WIN_GROUP, 2, BLOCKS, BLOCK)
    norm_scale = 1.0 / jnp.sqrt(jnp.float32(WINDOWS))
    row_batches = tile_rows.reshape(-1, TILES_DEV)
    col_batches = tile_cols.reshape(-1, TILES_DEV)

    def tile_batch(pair):
        left_block = jnp.take(blocks, pair[0], axis=4)
        right_block = jnp.take(blocks, pair[1], axis=4)
        real_part = jnp.einsum('gfwpka,gfwpkb->gkfab', left_block, right_block)
        imag_part = jnp.einsum('gfwka,gfwkb->gkfab', left_block[:, :, :, 0], right_block[:, :, :, 1])
        imag_part = imag_part - jnp.einsum('gfwka,gfwkb->gkfab', left_block[:, :, :, 1], right_block[:, :, :, 0])
        partial_value = jnp.stack([real_part, imag_part], axis=3) * norm_scale
        rounded = lax.optimization_barrier(partial_value.astype(jnp.bfloat16))
        return lax.optimization_barrier(jnp.sum(rounded.astype(jnp.float32), axis=0))
    stacked = lax.map(tile_batch, (row_batches, col_batches))
    return stacked.reshape(PAIR_TILES, FREQS, 2, BLOCK, BLOCK)
```

```python
import functools

import jax
import jax.numpy as jnp
from jax import lax
from jax.experimental import pallas as pl
from jax.experimental.pallas import tpu as pltpu
from jax.sharding import PartitionSpec as P

MESH = pl.DeviceIdType.MESH
BLOCK = 128
GATHERED = (2, 2, 4, 2, 8, 2, 4, 2, 16, 128)
STREAMS = (
    (0, 0, 3, "xyz"),
    (0, 3, 3, "yzx"),
    (0, 6, 2, "zxy"),
    (1, 0, 3, "xyz"),
    (1, 3, 2, "yzx"),
    (1, 5, 3, "zxy"),
)
UNROLL = 43


def whiten(spectra):
    power_sum = jnp.sum(spectra * spectra, axis=(1, 3), keepdims=True) / spectra.shape[1]
    return (spectra / jnp.maximum(jnp.sqrt(power_sum), 1.0)).astype(jnp.bfloat16)


def gather_kernel(
    src_ref, g, landed, spread, a2a_send, a2a_recv, send_sem, recv_sem, pass_send, pass_recv
):
    row, y, zh = lax.axis_index("row"), lax.axis_index("col"), lax.axis_index("win")
    x, zl, core = row // 4, (row // 2) % 2, row % 2
    here = {"x": x, "y": y, "z": zh * 2 + zl}

    def device(at, at_core):
        z = at["z"]
        return (at["x"] * 4 + (z % 2) * 2 + at_core, at["y"], z // 2)

    def shifted(axis, by):
        return here | {axis: (here[axis] + by) % 4}

    partner = device(here, 1 - core)
    me = (core * 4 + y) * 2 + zl

    def member(by):
        m = (me + by) % 16
        return m, (x * 4 + (m % 2) * 2 + m // 8, (m // 2) % 4, zh)

    barrier = pltpu.get_barrier_semaphore()
    others = [member(by)[1] for by in range(1, 16)]
    others += [device(shifted("x", 1), core), device(shifted("x", -1), core)]
    outer_z = here | {"z": (here["z"] + jnp.where(zl == 0, 3, 1)) % 4}
    others += [device(outer_z, core)]
    for other in others:
        pl.semaphore_signal(barrier, inc=1, device_id=other, device_id_type=MESH)
    pl.semaphore_wait(barrier, len(others))

    def swap(by):
        m, where = member(by)
        return pltpu.make_async_remote_copy(
            src_ref=src_ref.at[m],
            dst_ref=landed.at[me],
            send_sem=a2a_send.at[by],
            recv_sem=a2a_recv.at[by],
            device_id=where,
            device_id_type=MESH,
        )

    swaps = [swap(by) for by in range(1, 16)]
    for copy in swaps:
        copy.start()
    own = pltpu.make_async_copy(src_ref.at[me], landed.at[me], a2a_recv.at[0])
    own.start()
    own.wait()
    for copy in swaps:
        copy.wait_recv()
    for f in range(2):
        for p in range(2):
            for s in range(16):
                spread[f, p, pl.ds(s * 8, 8), :] = landed[s, f, p].astype(jnp.float32)
    for f in range(2):
        for p in range(2):
            for b in range(8):
                windows = spread[f, p, pl.ds(b, 16, stride=8), :]
                g[f, core, y, zl, b, p, x, zh] = windows.astype(jnp.bfloat16)

    every = slice(None)

    def box(stream, phase, at, part):
        f, b0, bn, order = STREAMS[stream]
        full = order[:phase]
        ys = every if "y" in full else at["y"]
        xs = every if "x" in full else at["x"]
        zls, zhs = (every, every) if "z" in full else (at["z"] % 2, at["z"] // 2)
        return g.at[f, core, ys, zls, pl.ds(b0, bn), part, xs, zhs]

    def ring(stream, phase, slot):
        axis = STREAMS[stream][3][phase]
        way, whose, part = ((1, 0, 0), (-1, 0, 1), (1, 0, 1), (-1, 0, 0), (1, -1, 0), (-1, 1, 1))[slot]
        ref = box(stream, phase, shifted(axis, whose), part)
        return pltpu.make_async_remote_copy(
            src_ref=ref,
            dst_ref=ref,
            send_sem=send_sem.at[stream, phase],
            recv_sem=recv_sem.at[stream, phase, slot],
            device_id=device(shifted(axis, way), core),
            device_id_type=MESH,
        )

    def arrived(stream, phase, slot):
        axis = STREAMS[stream][3][phase]
        way, whose, part = ((1, 0, 0), (-1, 0, 1), (1, 0, 1), (-1, 0, 0), (1, -1, 0), (-1, 1, 1))[slot]
        ref = box(stream, phase, shifted(axis, whose - way), part)
        pltpu.make_async_copy(ref, ref, recv_sem.at[stream, phase, slot]).wait()
        return ref

    def hand_over(stream, ref):
        pltpu.make_async_remote_copy(
            src_ref=ref,
            dst_ref=ref,
            send_sem=pass_send.at[stream],
            recv_sem=pass_recv.at[stream],
            device_id=partner,
            device_id_type=MESH,
        ).start()

    def start(stream, phase):
        for slot in range(4):
            ring(stream, phase, slot).start()
        if phase == 0:
            for part in range(2):
                hand_over(stream, box(stream, 0, here, part))

    def relay(stream, phase):
        for slot in range(2):
            ref = arrived(stream, phase, slot)
            ring(stream, phase, slot + 4).start()
            hand_over(stream, ref)

    def finish(stream, phase):
        for slot in range(2, 6):
            hand_over(stream, arrived(stream, phase, slot))

    early, late = range(3), range(3, 6)
    for group in (early, late):
        for s in group:
            start(s, 0)
    for group in (early, late):
        for s in group:
            relay(s, 0)
    for group in (early, late):
        for s in group:
            finish(s, 0)
            start(s, 1)
    for phase in (1, 2):
        for group in (early, late):
            for s in group:
                relay(s, phase)
            for s in group:
                finish(s, phase)
                if phase == 1:
                    start(s, 2)

    for copy in swaps:
        copy.wait_send()
    for s, (f, b0, bn, order) in enumerate(STREAMS):
        for phase in range(3):
            xs = slice(0, 1) if phase == 0 else every
            zs = slice(0, 1) if phase < 2 else every
            ref = g.at[f, core, pl.ds(0, 3), zs, pl.ds(b0, bn), :, xs, zs]
            pltpu.make_async_copy(ref, ref, send_sem.at[s, phase]).wait()
        ref = g.at[f, core, :, :, pl.ds(b0, bn)]
        pltpu.make_async_copy(ref, ref, pass_send.at[s]).wait()
        ref = g.at[f, 1 - core, :, :, pl.ds(b0, bn)]
        pltpu.make_async_copy(ref, ref, pass_recv.at[s]).wait()


def gather(source):
    return pl.pallas_call(
        gather_kernel,
        out_shape=pltpu.VMEM(GATHERED, jnp.bfloat16),
        in_specs=[pl.BlockSpec(memory_space=pltpu.VMEM)],
        out_specs=pl.BlockSpec(memory_space=pltpu.VMEM),
        scratch_shapes=[
            pltpu.VMEM((16, 2, 2, 8, BLOCK), jnp.bfloat16),
            pltpu.VMEM((2, 2, BLOCK, BLOCK), jnp.float32),
            pltpu.SemaphoreType.DMA((16,)),
            pltpu.SemaphoreType.DMA((16,)),
            pltpu.SemaphoreType.DMA((6, 3)),
            pltpu.SemaphoreType.DMA((6, 3, 6)),
            pltpu.SemaphoreType.DMA((6,)),
            pltpu.SemaphoreType.DMA((6,)),
        ],
        compiler_params=pltpu.CompilerParams(
            collective_id=0, has_side_effects=True, vmem_limit_bytes=32 << 20
        ),
    )(source)


def stack_kernel(rows_ref, cols_ref, g_ref, out_ref, held, sem):
    win = lax.axis_index("win")
    tiles = rows_ref.shape[0]
    norm = 1.0 / jnp.sqrt(jnp.float32(BLOCK))
    steps = tiles // UNROLL

    def put(f, step):
        slot = (f * steps + step) % 2
        return pltpu.make_async_copy(
            held.at[slot], out_ref.at[pl.ds(step * UNROLL, UNROLL), f], sem.at[slot]
        )

    for f in range(2):

        def body(step, carry):
            slot = (f * steps + step) % 2

            @pl.when(f * steps + step >= 2)
            def _():
                put(f, step).wait()

            for u in range(UNROLL):
                k = step * UNROLL + u
                turned = g_ref[f, rows_ref[k]].T
                left = jnp.where(win == 0, turned[:64], turned[64:])
                crossed = jnp.concatenate([-left[:, 128:], left[:, :128]], axis=1)
                both = jnp.dot(
                    jnp.concatenate([left, crossed], axis=0),
                    g_ref[f, cols_ref[k]],
                    preferred_element_type=jnp.float32,
                )
                both = both * norm
                held[slot, u, 0] = both[:64]
                held[slot, u, 1] = both[64:]
            put(f, step).start()
            return carry

        lax.fori_loop(0, steps, body, 0)
    put(1, steps - 2).wait()
    put(1, steps - 1).wait()


def stack_pairs(gathered, tile_rows, tile_cols):
    tiles = tile_rows.shape[0]
    return pl.pallas_call(
        stack_kernel,
        out_shape=jax.ShapeDtypeStruct((tiles, 2, 2, 64, BLOCK), jnp.float32),
        in_specs=[pl.BlockSpec(memory_space=pltpu.SMEM)] * 2 + [pl.BlockSpec(memory_space=pltpu.VMEM)],
        out_specs=pl.BlockSpec(memory_space=pl.ANY),
        scratch_shapes=[
            pltpu.VMEM((2, UNROLL, 2, 64, BLOCK), jnp.float32),
            pltpu.SemaphoreType.DMA((2,)),
        ],
        compiler_params=pltpu.CompilerParams(vmem_limit_bytes=30 << 20),
    )(tile_rows, tile_cols, gathered)


def on_device(spectra, tile_rows, tile_cols):
    whitened = whiten(spectra)[0, :, 0].reshape(2, 2, 16, 8, BLOCK)
    gathered = gather(jnp.transpose(whitened, (2, 0, 1, 3, 4)))
    return stack_pairs(gathered.reshape(2, 128, 256, BLOCK), tile_rows, tile_cols)


def solution(mesh):
    in_specs = (P("win", None, ("row", "col"), None, None), P(("row", "col")), P(("row", "col")))
    out_specs = P(("row", "col"), None, None, "win", None)
    return jax.shard_map(
        on_device, mesh=mesh, in_specs=in_specs, out_specs=out_specs, check_vma=False
    )
```

```python
import functools
import heapq

import jax
import jax.numpy as jnp
from jax import lax
from jax.experimental import pallas as pl
from jax.experimental.pallas import tpu as pltpu
from jax.sharding import PartitionSpec as P

MESH = pl.DeviceIdType.MESH
BLOCK = 128
GATHERED = (2, 4, 32, 2, 4, 4, 8, BLOCK)
STREAMS = ((0, 11, "xyz"), (11, 11, "yzx"), (22, 10, "zxy"))
OFFSETS = (0, 1, -1, 2)
SLOTS = ((1, 0, 0), (-1, 0, 1), (1, 0, 1), (-1, 0, 0), (1, -1, 0), (-1, 1, 1))
PIECES = tuple(
    (stream, phase, offset)
    for stream in range(3)
    for phase in range(3)
    for offset in (OFFSETS if phase else (0,))
)
UNROLL = 43


def plan(hop=1.6, rate=46.5e3):
    needs = {}
    for piece in PIECES:
        stream, phase, offset = piece
        for part in range(2):
            if phase == 0 or (phase == 1 and offset == 0):
                need = set()
            elif phase == 1:
                need = {((stream, 0, 0), offset, part)}
            elif offset == 0:
                need = {((stream, 0, 0), by, part) for by in OFFSETS[1:]}
            else:
                need = {((stream, 1, by), offset, part) for by in OFFSETS}
            needs[piece, part] = need
    free, heap, have, started = {}, [], set(), set()

    def send(piece, slot, now):
        stream, phase, offset = piece
        _, units, order = STREAMS[stream]
        link = (order[phase], SLOTS[slot][0])
        size = units * 2048 * (4 if phase == 2 else 1)
        begin = max(now, free.get(link, 0.0))
        free[link] = begin + size / rate
        heapq.heappush(heap, (free[link] + hop, len(started), piece, slot))
        started.add((piece, slot))

    def ready(now):
        out = []
        for phase in range(3):
            for slot in range(4):
                for piece in PIECES:
                    if piece[1] == phase and (piece, slot) not in started:
                        if needs[piece, SLOTS[slot][2]] <= have:
                            send(piece, slot, now)
                            out.append((piece, slot))
        return out

    steps = [(None, ready(0.0))]
    while heap:
        now, _, piece, slot = heapq.heappop(heap)
        way, whose, part = SLOTS[slot]
        out = []
        if slot < 2:
            send(piece, slot + 4, now)
            out.append((piece, slot + 4))
        have.add((piece, {-1: -1, 1: 1, -2: 2, 2: 2}[whose - way], part))
        steps.append(((piece, slot), out + ready(now)))
    return steps, now


def gather_kernel(x_ref, g, raw, source, landed, spread, load, a2a_send, a2a_recv, sent, got, passed, taken):
    row, y, zh = lax.axis_index("row"), lax.axis_index("col"), lax.axis_index("win")
    x, zl, core = row // 4, (row // 2) % 2, row % 2
    z = zh * 2 + zl
    here = {"x": x, "y": y, "z": z}

    def device(at, at_core):
        return (at["x"] * 4 + (at["z"] % 2) * 2 + at_core, at["y"], at["z"] // 2)

    def shifted(axis, by):
        return here | {axis: (here[axis] + by) % 4}

    me = core * 4 + y

    def member(by):
        m = (me + by) % 8
        return m, device(here | {"y": m % 4}, m // 4)

    fetch = pltpu.make_async_copy(x_ref, raw, load)
    fetch.start()
    barrier = pltpu.get_barrier_semaphore()
    others = [member(by)[1] for by in range(1, 8)]
    others += [device(shifted(axis, by), core) for axis in "xz" for by in (1, -1)]
    for other in others:
        pl.semaphore_signal(barrier, inc=1, device_id=other, device_id_type=MESH)
    fetch.wait()
    for m in range(8):
        values = [[raw[f, pl.ds(m * 32 + p, 16, stride=2), :] for p in range(2)] for f in range(2)]
        power = sum(v * v for pair in values for v in pair) / 2
        scale = jnp.maximum(jnp.sqrt(power), 1.0)
        for f in range(2):
            for p in range(2):
                source[m, f, p] = (values[f][p] / scale).astype(jnp.bfloat16)
    pl.semaphore_wait(barrier, len(others))

    def swap(by):
        m, where = member(by)
        return pltpu.make_async_remote_copy(
            src_ref=source.at[m],
            dst_ref=landed.at[me],
            send_sem=a2a_send.at[by],
            recv_sem=a2a_recv.at[by],
            device_id=where,
            device_id_type=MESH,
        )

    swaps = [swap(by) for by in range(1, 8)]
    for copy in swaps:
        copy.start()
    own = pltpu.make_async_copy(source.at[me], landed.at[me], a2a_recv.at[0])
    own.start()
    own.wait()
    for copy in swaps:
        copy.wait_recv()
    for f in range(2):
        for p in range(2):
            for s in range(8):
                spread[f, p, pl.ds(s * 16, 16), :] = landed[s, f, p].astype(jnp.float32)
    for f in range(2):
        for p in range(2):
            for b in range(16):
                windows = spread[f, p, pl.ds(b, 8, stride=16), :]
                g[core, y, b * 2 + f, p, x, z] = windows.astype(jnp.bfloat16)

    every = slice(None)

    def box(piece, by, part):
        stream, phase, offset = piece
        first, units, order = STREAMS[stream]
        at = dict(here)
        at[order[phase]] = (here[order[phase]] + by) % 4
        if phase:
            at[order[phase - 1]] = (here[order[phase - 1]] + offset) % 4
        if phase == 2:
            at[order[0]] = every
        return g.at[core, at["y"], pl.ds(first, units), part, at["x"], at["z"]]

    def index(piece):
        return PIECES.index(piece)

    def launch(piece, slot):
        way, whose, part = SLOTS[slot]
        ref = box(piece, whose, part)
        pltpu.make_async_remote_copy(
            src_ref=ref,
            dst_ref=ref,
            send_sem=sent.at[piece[0], piece[1]],
            recv_sem=got.at[index(piece), slot],
            device_id=device(shifted(STREAMS[piece[0]][2][piece[1]], way), core),
            device_id_type=MESH,
        ).start()

    def hand_over(ref):
        pltpu.make_async_remote_copy(
            src_ref=ref,
            dst_ref=ref,
            send_sem=passed,
            recv_sem=taken,
            device_id=device(here, 1 - core),
            device_id_type=MESH,
        ).start()

    for received, copies in plan()[0]:
        if received is not None:
            piece, slot = received
            way, whose, part = SLOTS[slot]
            ref = box(piece, whose - way, part)
            pltpu.make_async_copy(ref, ref, got.at[index(piece), slot]).wait()
        for copy in copies:
            launch(*copy)
        hand_over(g.at[core, y, :, :, x, z] if received is None else ref)

    for copy in swaps:
        copy.wait_send()
    for s, (first, units, _) in enumerate(STREAMS):
        for phase in range(3):
            xs = slice(0, 1) if phase == 0 else every
            zs = slice(0, 1) if phase < 2 else every
            ref = g.at[core, pl.ds(0, 3), pl.ds(first, units), :, xs, zs]
            pltpu.make_async_copy(ref, ref, sent.at[s, phase]).wait()
    pltpu.make_async_copy(g.at[core], g.at[core], passed).wait()
    pltpu.make_async_copy(g.at[1 - core], g.at[1 - core], taken).wait()


def gather(spectra):
    return pl.pallas_call(
        gather_kernel,
        out_shape=pltpu.VMEM(GATHERED, jnp.bfloat16),
        in_specs=[pl.BlockSpec(memory_space=pltpu.HBM)],
        out_specs=pl.BlockSpec(memory_space=pltpu.VMEM),
        scratch_shapes=[
            pltpu.VMEM((2, 256, BLOCK), jnp.float32),
            pltpu.VMEM((8, 2, 2, 16, BLOCK), jnp.bfloat16),
            pltpu.VMEM((8, 2, 2, 16, BLOCK), jnp.bfloat16),
            pltpu.VMEM((2, 2, BLOCK, BLOCK), jnp.float32),
            pltpu.SemaphoreType.DMA,
            pltpu.SemaphoreType.DMA((8,)),
            pltpu.SemaphoreType.DMA((8,)),
            pltpu.SemaphoreType.DMA((3, 3)),
            pltpu.SemaphoreType.DMA((len(PIECES), 6)),
            pltpu.SemaphoreType.DMA,
            pltpu.SemaphoreType.DMA,
        ],
        compiler_params=pltpu.CompilerParams(
            collective_id=0, has_side_effects=True, vmem_limit_bytes=32 << 20
        ),
    )(spectra)


def stack_kernel(rows_ref, cols_ref, g_ref, out_ref, held, sem):
    win = lax.axis_index("win")
    tiles = rows_ref.shape[0]
    norm = 1.0 / jnp.sqrt(jnp.float32(BLOCK))
    steps = tiles // UNROLL

    def put(f, step):
        slot = (f * steps + step) % 2
        return pltpu.make_async_copy(
            held.at[slot], out_ref.at[pl.ds(step * UNROLL, UNROLL), f], sem.at[slot]
        )

    for f in range(2):

        def body(step, carry):
            slot = (f * steps + step) % 2

            @pl.when(f * steps + step >= 2)
            def _():
                put(f, step).wait()

            for u in range(UNROLL):
                k = step * UNROLL + u
                turned = g_ref[rows_ref[k], f].T
                left = jnp.where(win == 0, turned[:64], turned[64:])
                crossed = jnp.concatenate([-left[:, 128:], left[:, :128]], axis=1)
                both = jnp.dot(
                    jnp.concatenate([left, crossed], axis=0),
                    g_ref[cols_ref[k], f],
                    preferred_element_type=jnp.float32,
                )
                both = both * norm
                held[slot, u, 0] = both[:64]
                held[slot, u, 1] = both[64:]
            put(f, step).start()
            return carry

        lax.fori_loop(0, steps, body, 0)
    put(1, steps - 2).wait()
    put(1, steps - 1).wait()


def stack_pairs(gathered, tile_rows, tile_cols):
    tiles = tile_rows.shape[0]
    return pl.pallas_call(
        stack_kernel,
        out_shape=jax.ShapeDtypeStruct((tiles, 2, 2, 64, BLOCK), jnp.float32),
        in_specs=[pl.BlockSpec(memory_space=pltpu.SMEM)] * 2 + [pl.BlockSpec(memory_space=pltpu.VMEM)],
        out_specs=pl.BlockSpec(memory_space=pl.ANY),
        scratch_shapes=[
            pltpu.VMEM((2, UNROLL, 2, 64, BLOCK), jnp.float32),
            pltpu.SemaphoreType.DMA((2,)),
        ],
        compiler_params=pltpu.CompilerParams(vmem_limit_bytes=30 << 20),
    )(tile_rows, tile_cols, gathered)


def on_device(spectra, tile_rows, tile_cols):
    values = spectra[0, :, 0].reshape(2, 2, BLOCK, BLOCK)
    gathered = gather(jnp.transpose(values, (0, 2, 1, 3)).reshape(2, 2 * BLOCK, BLOCK))
    return stack_pairs(gathered.reshape(BLOCK, 2, 2 * BLOCK, BLOCK), tile_rows, tile_cols)


def solution(mesh):
    in_specs = (P("win", None, ("row", "col"), None, None), P(("row", "col")), P(("row", "col")))
    out_specs = P(("row", "col"), None, None, "win", None)
    return jax.shard_map(
        on_device, mesh=mesh, in_specs=in_specs, out_specs=out_specs, check_vma=False
    )
```

```python
import functools
import heapq

import jax
import jax.numpy as jnp
from jax import lax
from jax.experimental import pallas as pl
from jax.experimental.pallas import tpu as pltpu
from jax.sharding import PartitionSpec as P

MESH = pl.DeviceIdType.MESH
BLOCK = 128
GATHERED = (2, 4, 32, 2, 4, 4, 8, BLOCK)
STREAMS = ((0, 11, "xyz"), (11, 11, "yzx"), (22, 10, "zxy"))
OFFSETS = (0, 1, -1, 2)
SLOTS = ((1, 0, 0), (-1, 0, 1), (1, 0, 1), (-1, 0, 0), (1, -1, 0), (-1, 1, 1))


def cut_pieces(last=3):
    pieces = []
    for stream, (first, units, _) in enumerate(STREAMS):
        pieces.append((stream, 0, 0, None, first, units))
        for offset in OFFSETS:
            pieces.append((stream, 1, offset, None, first, units))
        for offset in OFFSETS:
            for before in OFFSETS if offset == 0 else (None,):
                parts = last if offset == 2 else 1
                edges = [first + units * i // parts for i in range(parts + 1)]
                for lo, hi in zip(edges, edges[1:]):
                    pieces.append((stream, 2, offset, before, lo, hi - lo))
    return tuple(pieces)


PIECES = cut_pieces()
CUTS = (5, 12, 20, 24, 24, 20, 14, 10)


def plan(hop=1.6, rate=46.5e3):
    needs = {}
    for piece in PIECES:
        stream, phase, offset, before = piece[:4]
        for part in range(2):
            if phase == 1 and offset:
                need = {(stream, 0, 0, offset, part)}
            elif phase == 2 and offset:
                need = {(stream, 1, by, offset, part) for by in OFFSETS}
            elif phase == 2 and before:
                need = {(stream, 0, 0, before, part)}
            else:
                need = set()
            needs[piece, part] = need
    free, heap, have, started = {}, [], set(), set()

    def send(piece, slot, now):
        stream, phase, _, before, _, units = piece
        link = (STREAMS[stream][2][phase], SLOTS[slot][0])
        size = units * 2048 * (4 if phase == 2 and before is None else 1)
        begin = max(now, free.get(link, 0.0))
        free[link] = begin + size / rate
        heapq.heappush(heap, (free[link] + hop, len(started), piece, slot))
        started.add((piece, slot))

    def ready(now):
        out = []
        for phase in range(3):
            for slot in range(4):
                for piece in PIECES:
                    if piece[1] == phase and (piece, slot) not in started:
                        if needs[piece, SLOTS[slot][2]] <= have:
                            send(piece, slot, now)
                            out.append((piece, slot))
        return out

    steps = [(None, ready(0.0))]
    while heap:
        now, _, piece, slot = heapq.heappop(heap)
        way, whose, part = SLOTS[slot]
        out = []
        if slot < 2:
            send(piece, slot + 4, now)
            out.append((piece, slot + 4))
        have.add((*piece[:3], {-1: -1, 1: 1, -2: 2, 2: 2}[whose - way], part))
        steps.append(((piece, slot), out + ready(now)))
    return steps, now


def gather_kernel(x_ref, g, raw, source, landed, spread, load, a2a_send, a2a_recv, sent, got, passed, taken):
    row, y, zh = lax.axis_index("row"), lax.axis_index("col"), lax.axis_index("win")
    x, zl, core = row // 4, (row // 2) % 2, row % 2
    z = zh * 2 + zl
    here = {"x": x, "y": y, "z": z}

    def device(at, at_core):
        return (at["x"] * 4 + (at["z"] % 2) * 2 + at_core, at["y"], at["z"] // 2)

    def shifted(axis, by):
        return here | {axis: (here[axis] + by) % 4}

    me = core * 4 + y

    def member(by):
        m = (me + by) % 8
        return m, device(here | {"y": m % 4}, m // 4)

    fetch = pltpu.make_async_copy(x_ref, raw, load)
    fetch.start()
    barrier = pltpu.get_barrier_semaphore()
    others = [member(by)[1] for by in range(1, 8)]
    others += [device(shifted(axis, by), core) for axis in "xz" for by in (1, -1)]
    for other in others:
        pl.semaphore_signal(barrier, inc=1, device_id=other, device_id_type=MESH)
    fetch.wait()
    for m in range(8):
        values = [[raw[f, pl.ds(m * 32 + p, 16, stride=2), :] for p in range(2)] for f in range(2)]
        power = sum(v * v for pair in values for v in pair) / 2
        scale = jnp.maximum(jnp.sqrt(power), 1.0)
        for f in range(2):
            for p in range(2):
                source[m, f, p] = (values[f][p] / scale).astype(jnp.bfloat16)
    pl.semaphore_wait(barrier, len(others))

    def swap(by):
        m, where = member(by)
        return pltpu.make_async_remote_copy(
            src_ref=source.at[m],
            dst_ref=landed.at[me],
            send_sem=a2a_send.at[by],
            recv_sem=a2a_recv.at[by],
            device_id=where,
            device_id_type=MESH,
        )

    swaps = [swap(by) for by in range(1, 8)]
    for copy in swaps:
        copy.start()
    own = pltpu.make_async_copy(source.at[me], landed.at[me], a2a_recv.at[0])
    own.start()
    own.wait()
    for copy in swaps:
        copy.wait_recv()
    for f in range(2):
        for p in range(2):
            for s in range(8):
                spread[f, p, pl.ds(s * 16, 16), :] = landed[s, f, p].astype(jnp.float32)
    for f in range(2):
        for p in range(2):
            for b in range(16):
                windows = spread[f, p, pl.ds(b, 8, stride=16), :]
                g[core, y, b * 2 + f, p, x, z] = windows.astype(jnp.bfloat16)

    every = slice(None)

    def box(piece, by, part):
        stream, phase, offset, before, first, units = piece
        order = STREAMS[stream][2]
        at = dict(here)
        at[order[phase]] = (here[order[phase]] + by) % 4
        if phase:
            at[order[phase - 1]] = (here[order[phase - 1]] + offset) % 4
        if phase == 2:
            at[order[0]] = every if before is None else (here[order[0]] + before) % 4
        return g.at[core, at["y"], pl.ds(first, units), part, at["x"], at["z"]]

    def index(piece):
        return PIECES.index(piece)

    def launch(piece, slot):
        way, whose, part = SLOTS[slot]
        ref = box(piece, whose, part)
        pltpu.make_async_remote_copy(
            src_ref=ref,
            dst_ref=ref,
            send_sem=sent.at[piece[0], piece[1]],
            recv_sem=got.at[index(piece), slot],
            device_id=device(shifted(STREAMS[piece[0]][2][piece[1]], way), core),
            device_id_type=MESH,
        ).start()

    def hand_over(ref):
        pltpu.make_async_remote_copy(
            src_ref=ref,
            dst_ref=ref,
            send_sem=passed,
            recv_sem=taken,
            device_id=device(here, 1 - core),
            device_id_type=MESH,
        ).start()

    for received, copies in plan()[0]:
        if received is not None:
            piece, slot = received
            way, whose, part = SLOTS[slot]
            ref = box(piece, whose - way, part)
            pltpu.make_async_copy(ref, ref, got.at[index(piece), slot]).wait()
        for copy in copies:
            launch(*copy)
        hand_over(g.at[core, y, :, :, x, z] if received is None else ref)

    for copy in swaps:
        copy.wait_send()
    for s, (first, units, _) in enumerate(STREAMS):
        for phase in range(3):
            xs = slice(0, 1) if phase == 0 else every
            zs = slice(0, 1) if phase < 2 else every
            ref = g.at[core, pl.ds(0, 3), pl.ds(first, units), :, xs, zs]
            pltpu.make_async_copy(ref, ref, sent.at[s, phase]).wait()
    pltpu.make_async_copy(g.at[core], g.at[core], passed).wait()
    pltpu.make_async_copy(g.at[1 - core], g.at[1 - core], taken).wait()


def gather(spectra):
    return pl.pallas_call(
        gather_kernel,
        out_shape=pltpu.VMEM(GATHERED, jnp.bfloat16),
        in_specs=[pl.BlockSpec(memory_space=pltpu.HBM)],
        out_specs=pl.BlockSpec(memory_space=pltpu.VMEM),
        scratch_shapes=[
            pltpu.VMEM((2, 256, BLOCK), jnp.float32),
            pltpu.VMEM((8, 2, 2, 16, BLOCK), jnp.bfloat16),
            pltpu.VMEM((8, 2, 2, 16, BLOCK), jnp.bfloat16),
            pltpu.VMEM((2, 2, BLOCK, BLOCK), jnp.float32),
            pltpu.SemaphoreType.DMA,
            pltpu.SemaphoreType.DMA((8,)),
            pltpu.SemaphoreType.DMA((8,)),
            pltpu.SemaphoreType.DMA((3, 3)),
            pltpu.SemaphoreType.DMA((len(PIECES), 6)),
            pltpu.SemaphoreType.DMA,
            pltpu.SemaphoreType.DMA,
        ],
        compiler_params=pltpu.CompilerParams(
            collective_id=0, has_side_effects=True, vmem_limit_bytes=32 << 20
        ),
    )(spectra)


def stack_kernel(rows_ref, cols_ref, g_ref, out_ref, held, sem):
    win = lax.axis_index("win")
    norm = 1.0 / jnp.sqrt(jnp.float32(BLOCK))
    puts = []
    for f in range(2):
        first = 0
        for tiles in CUTS if f == 0 else CUTS[::-1]:
            for k in range(first, first + tiles):
                turned = g_ref[rows_ref[k], f].T
                left = jnp.where(win == 0, turned[:64], turned[64:])
                crossed = jnp.concatenate([-left[:, 128:], left[:, :128]], axis=1)
                both = jnp.dot(
                    jnp.concatenate([left, crossed], axis=0),
                    g_ref[cols_ref[k], f],
                    preferred_element_type=jnp.float32,
                )
                both = both * norm
                held[f, k, 0] = both[:64]
                held[f, k, 1] = both[64:]
            put = pltpu.make_async_copy(
                held.at[f, pl.ds(first, tiles)], out_ref.at[pl.ds(first, tiles), f], sem.at[len(puts)]
            )
            put.start()
            puts.append(put)
            first += tiles
    for put in puts:
        put.wait()


def stack_pairs(gathered, tile_rows, tile_cols):
    tiles = tile_rows.shape[0]
    return pl.pallas_call(
        stack_kernel,
        out_shape=jax.ShapeDtypeStruct((tiles, 2, 2, 64, BLOCK), jnp.float32),
        in_specs=[pl.BlockSpec(memory_space=pltpu.SMEM)] * 2 + [pl.BlockSpec(memory_space=pltpu.VMEM)],
        out_specs=pl.BlockSpec(memory_space=pl.ANY),
        scratch_shapes=[
            pltpu.VMEM((2, tiles, 2, 64, BLOCK), jnp.float32),
            pltpu.SemaphoreType.DMA((2 * len(CUTS),)),
        ],
        compiler_params=pltpu.CompilerParams(vmem_limit_bytes=24 << 20),
    )(tile_rows, tile_cols, gathered)


def on_device(spectra, tile_rows, tile_cols):
    values = spectra[0, :, 0].reshape(2, 2, BLOCK, BLOCK)
    values = jnp.transpose(values, (0, 2, 1, 3)).reshape(2, 2 * BLOCK, BLOCK)
    gathered = gather(pltpu.with_memory_space_constraint(values, pltpu.HBM))
    return stack_pairs(gathered.reshape(BLOCK, 2, 2 * BLOCK, BLOCK), tile_rows, tile_cols)


def solution(mesh):
    in_specs = (P("win", None, ("row", "col"), None, None), P(("row", "col")), P(("row", "col")))
    out_specs = P(("row", "col"), None, None, "win", None)
    return jax.shard_map(
        on_device, mesh=mesh, in_specs=in_specs, out_specs=out_specs, check_vma=False
    )
```

```python
import heapq
import itertools
import math

import jax
import jax.numpy as jnp
from jax import lax
from jax.experimental import pallas as pl
from jax.experimental.pallas import tpu as pltpu
from jax.sharding import PartitionSpec as P

MESH = pl.DeviceIdType.MESH
BLOCK = 128
GATHERED = (2, 4, 32, 2, 4, 4, 8, BLOCK)
STREAMS = ((0, 11, "xyz"), (11, 11, "yzx"), (22, 10, "zxy"))
OFFSETS = (0, 1, -1, 2)
SLOTS = ((1, 0, 0), (-1, 0, 1), (1, 0, 1), (-1, 0, 0), (1, -1, 0), (-1, 1, 1))


def cut_pieces():
    pieces = []
    for stream in range(len(STREAMS)):
        pieces.append((stream, 0, 0, None))
        pieces += [(stream, 1, offset, None) for offset in OFFSETS]
        pieces += [(stream, 2, 0, before) for before in OFFSETS]
        pieces += [(stream, 2, offset, None) for offset in OFFSETS[1:]]
    return tuple(pieces)


def group_of(piece, slot):
    stream, phase, offset, before = piece
    if slot < 2:
        return (piece, slot)
    if phase == 0:
        return (piece, min(slot, 4))
    if phase == 1:
        return (stream, 1, slot // 2)
    if offset == 0 and before:
        return (stream, 2)
    if offset == 2:
        return (piece, slot // 2)
    return (piece, 2)


PIECES = cut_pieces()
GROUPS = {}
for _piece in PIECES:
    for _slot in range(6):
        GROUPS.setdefault(group_of(_piece, _slot), []).append((_piece, _slot))
ORDER = list(GROUPS)
CUTS = (5, 12, 20, 24, 24, 20, 14, 10)


def group_stream(group):
    return GROUPS[group][0][0][0]


def plan(hop=3.5, rate=46.5e3):
    needs = {}
    for piece in PIECES:
        stream, phase, offset, before = piece
        for part in range(2):
            if phase == 1 and offset:
                need = {(stream, 0, 0, offset, part)}
            elif phase == 2 and offset:
                need = {(stream, 1, by, offset, part) for by in OFFSETS}
            elif phase == 2 and before:
                need = {(stream, 0, 0, before, part)}
            else:
                need = set()
            needs[piece, part] = need
    free, heap, have, started = {}, [], set(), set()
    missing = {group: len(copies) for group, copies in GROUPS.items()}

    def send(piece, slot, now):
        stream, phase, _, before = piece
        link = (STREAMS[stream][2][phase], SLOTS[slot][0])
        size = STREAMS[stream][1] * 2048 * (4 if phase == 2 and before is None else 1)
        begin = max(now, free.get(link, 0.0))
        free[link] = begin + size / rate
        heapq.heappush(heap, (free[link] + hop, len(started), piece, slot))
        started.add((piece, slot))

    def ready(now):
        out = []
        for phase in range(3):
            for slot in range(4):
                for piece in PIECES:
                    if piece[1] == phase and (piece, slot) not in started:
                        if needs[piece, SLOTS[slot][2]] <= have:
                            send(piece, slot, now)
                            out.append((piece, slot))
        return out

    steps = [(None, ready(0.0))]
    while heap:
        now, _, piece, slot = heapq.heappop(heap)
        group = group_of(piece, slot)
        missing[group] -= 1
        if missing[group]:
            continue
        out = []
        for piece, slot in GROUPS[group]:
            way, whose, part = SLOTS[slot]
            if slot < 2:
                send(piece, slot + 4, now)
                out.append((piece, slot + 4))
            have.add((*piece[:3], {-1: -1, 1: 1, -2: 2, 2: 2}[whose - way], part))
        steps.append((group, out + ready(now)))
    return steps, now


def gather_kernel(x_ref, g, raw, source, landed, spread, load, a2a_send, a2a_recv, sent, got, passed, taken):
    row, y, zh = lax.axis_index("row"), lax.axis_index("col"), lax.axis_index("win")
    x, zl, core = row // 4, (row // 2) % 2, row % 2
    z = zh * 2 + zl
    here = {"x": x, "y": y, "z": z}

    def device(at, at_core):
        return (at["x"] * 4 + (at["z"] % 2) * 2 + at_core, at["y"], at["z"] // 2)

    def shifted(axis, by):
        return here | {axis: (here[axis] + by) % 4}

    me = core * 4 + y

    def member(by):
        m = (me + by) % 8
        return m, device(here | {"y": m % 4}, m // 4)

    fetch = pltpu.make_async_copy(x_ref, raw, load)
    fetch.start()
    barrier = pltpu.get_barrier_semaphore()

    def greet(other):
        pl.semaphore_signal(barrier, inc=1, device_id=other, device_id_type=MESH)

    def greet_member(by, carry):
        greet(member(by)[1])
        return carry

    def greet_neighbours(i, carry):
        greet(device(shifted("x", 1 + 2 * i), core))
        greet(device(shifted("z", 1 + 2 * i), core))
        return carry

    lax.fori_loop(1, 8, greet_member, 0)
    lax.fori_loop(0, 2, greet_neighbours, 0)
    fetch.wait()
    for m in range(8):
        values = [[raw[f, pl.ds(m * 32 + p, 16, stride=2), :] for p in range(2)] for f in range(2)]
        power = sum(v * v for pair in values for v in pair) / 2
        scale = jnp.maximum(jnp.sqrt(power), 1.0)
        for f in range(2):
            for p in range(2):
                source[m, f, p] = (values[f][p] / scale).astype(jnp.bfloat16)
    pl.semaphore_wait(barrier, 11)

    def swap(by):
        m, where = member(by)
        return pltpu.make_async_remote_copy(
            src_ref=source.at[m],
            dst_ref=landed.at[me],
            send_sem=a2a_send,
            recv_sem=a2a_recv,
            device_id=where,
            device_id_type=MESH,
        )

    def start_swap(by, carry):
        swap(by).start()
        return carry

    lax.fori_loop(1, 8, start_swap, 0)
    own = pltpu.make_async_copy(source.at[me], landed.at[me], load)
    own.start()
    own.wait()
    seven = landed.at[pl.ds(0, 7)]
    pltpu.make_async_copy(seven, seven, a2a_recv).wait()
    for f in range(2):
        for p in range(2):
            for s in range(8):
                spread[f, p, pl.ds(s * 16, 16), :] = landed[s, f, p].astype(jnp.float32)
    for f in range(2):
        for p in range(2):
            for b in range(16):
                windows = spread[f, p, pl.ds(b, 8, stride=16), :]
                g[core, y, b * 2 + f, p, x, z] = windows.astype(jnp.bfloat16)

    every = slice(None)

    def box(piece, by, part):
        stream, phase, offset, before = piece
        first, units, order = STREAMS[stream]
        at = dict(here)
        at[order[phase]] = (here[order[phase]] + by) % 4
        if phase:
            at[order[phase - 1]] = (here[order[phase - 1]] + offset) % 4
        if phase == 2:
            at[order[0]] = every if before is None else (here[order[0]] + before) % 4
        return g.at[core, at["y"], pl.ds(first, units), part, at["x"], at["z"]]

    def any_boxes(stream, count):
        first, units, _ = STREAMS[stream]
        ys, xs, zs, parts = next(
            dims
            for dims in itertools.product(range(1, 5), range(1, 5), range(1, 5), (1, 2))
            if math.prod(dims) == count
        )
        return g.at[core, pl.ds(0, ys), pl.ds(first, units), pl.ds(0, parts), pl.ds(0, xs), pl.ds(0, zs)]

    def launch(piece, slot):
        way, whose, part = SLOTS[slot]
        ref = box(piece, whose, part)
        pltpu.make_async_remote_copy(
            src_ref=ref,
            dst_ref=ref,
            send_sem=sent.at[piece[0], piece[1]],
            recv_sem=got.at[ORDER.index(group_of(piece, slot))],
            device_id=device(shifted(STREAMS[piece[0]][2][piece[1]], way), core),
            device_id_type=MESH,
        ).start()

    def hand_over(ref):
        pltpu.make_async_remote_copy(
            src_ref=ref,
            dst_ref=ref,
            send_sem=passed,
            recv_sem=taken,
            device_id=device(here, 1 - core),
            device_id_type=MESH,
        ).start()

    for group, copies in plan()[0]:
        refs = [g.at[core, y, :, :, x, z]]
        if group is not None:
            refs, count = [], 0
            for piece, slot in GROUPS[group]:
                way, whose, part = SLOTS[slot]
                refs.append(box(piece, whose - way, part))
                count += 4 if piece[1] == 2 and piece[3] is None else 1
            ref = refs[0] if len(refs) == 1 else any_boxes(group_stream(group), count)
            pltpu.make_async_copy(ref, ref, got.at[ORDER.index(group)]).wait()
        for copy in copies:
            launch(*copy)
        for ref in refs:
            hand_over(ref)

    pltpu.make_async_copy(seven, seven, a2a_send).wait()
    for s, (first, units, _) in enumerate(STREAMS):
        for phase in range(3):
            xs = slice(0, 1) if phase == 0 else every
            zs = slice(0, 1) if phase < 2 else every
            ref = g.at[core, pl.ds(0, 3), pl.ds(first, units), :, xs, zs]
            pltpu.make_async_copy(ref, ref, sent.at[s, phase]).wait()
    pltpu.make_async_copy(g.at[core], g.at[core], passed).wait()
    pltpu.make_async_copy(g.at[1 - core], g.at[1 - core], taken).wait()


def gather(spectra):
    return pl.pallas_call(
        gather_kernel,
        out_shape=pltpu.VMEM(GATHERED, jnp.bfloat16),
        in_specs=[pl.BlockSpec(memory_space=pltpu.HBM)],
        out_specs=pl.BlockSpec(memory_space=pltpu.VMEM),
        scratch_shapes=[
            pltpu.VMEM((2, 256, BLOCK), jnp.float32),
            pltpu.VMEM((8, 2, 2, 16, BLOCK), jnp.bfloat16),
            pltpu.VMEM((8, 2, 2, 16, BLOCK), jnp.bfloat16),
            pltpu.VMEM((2, 2, BLOCK, BLOCK), jnp.float32),
            pltpu.SemaphoreType.DMA,
            pltpu.SemaphoreType.DMA,
            pltpu.SemaphoreType.DMA,
            pltpu.SemaphoreType.DMA((3, 3)),
            pltpu.SemaphoreType.DMA((len(ORDER),)),
            pltpu.SemaphoreType.DMA,
            pltpu.SemaphoreType.DMA,
        ],
        compiler_params=pltpu.CompilerParams(
            collective_id=0, has_side_effects=True, vmem_limit_bytes=32 << 20
        ),
    )(spectra)


def stack_kernel(rows_ref, cols_ref, g_ref, out_ref, held, sem):
    win = lax.axis_index("win")
    norm = 1.0 / jnp.sqrt(jnp.float32(BLOCK))
    for f in range(2):
        first = 0
        for tiles in CUTS if f == 0 else CUTS[::-1]:
            for k in range(first, first + tiles):
                turned = g_ref[rows_ref[k], f].T
                left = jnp.where(win == 0, turned[:64], turned[64:])
                crossed = jnp.concatenate([-left[:, 128:], left[:, :128]], axis=1)
                both = jnp.dot(
                    jnp.concatenate([left, crossed], axis=0),
                    g_ref[cols_ref[k], f],
                    preferred_element_type=jnp.float32,
                )
                both = both * norm
                held[f, k, 0] = both[:64]
                held[f, k, 1] = both[64:]
            put = pltpu.make_async_copy(
                held.at[f, pl.ds(first, tiles)], out_ref.at[pl.ds(first, tiles), f], sem
            )
            put.start()
            first += tiles
    pltpu.make_async_copy(held, held, sem).wait()


def stack_pairs(gathered, tile_rows, tile_cols):
    tiles = tile_rows.shape[0]
    return pl.pallas_call(
        stack_kernel,
        out_shape=jax.ShapeDtypeStruct((tiles, 2, 2, 64, BLOCK), jnp.float32),
        in_specs=[pl.BlockSpec(memory_space=pltpu.SMEM)] * 2 + [pl.BlockSpec(memory_space=pltpu.VMEM)],
        out_specs=pl.BlockSpec(memory_space=pl.ANY),
        scratch_shapes=[
            pltpu.VMEM((2, tiles, 2, 64, BLOCK), jnp.float32),
            pltpu.SemaphoreType.DMA,
        ],
        compiler_params=pltpu.CompilerParams(vmem_limit_bytes=24 << 20),
    )(tile_rows, tile_cols, gathered)


def on_device(spectra, tile_rows, tile_cols):
    values = spectra[0, :, 0].reshape(2, 2, BLOCK, BLOCK)
    values = jnp.transpose(values, (0, 2, 1, 3)).reshape(2, 2 * BLOCK, BLOCK)
    gathered = gather(pltpu.with_memory_space_constraint(values, pltpu.HBM))
    return stack_pairs(gathered.reshape(BLOCK, 2, 2 * BLOCK, BLOCK), tile_rows, tile_cols)


def solution(mesh):
    in_specs = (P("win", None, ("row", "col"), None, None), P(("row", "col")), P(("row", "col")))
    out_specs = P(("row", "col"), None, None, "win", None)
    return jax.shard_map(
        on_device, mesh=mesh, in_specs=in_specs, out_specs=out_specs, check_vma=False
    )
```

```python
import heapq
import itertools
import math

import jax
import jax.numpy as jnp
from jax import lax
from jax.experimental import pallas as pl
from jax.experimental.pallas import tpu as pltpu
from jax.sharding import PartitionSpec as P

MESH = pl.DeviceIdType.MESH
BLOCK = 128
GATHERED = (2, 4, 32, 2, 4, 4, 8, BLOCK)
STREAMS = ((0, 11, "xyz"), (11, 11, "yzx"), (22, 10, "zxy"))
OFFSETS = (0, 1, -1, 2)
SLOTS = ((1, 0, 0), (-1, 0, 1), (1, 0, 1), (-1, 0, 0), (1, -1, 0), (-1, 1, 1))


def cut_pieces(last=3):
    pieces = []
    for stream, (first, units, _) in enumerate(STREAMS):
        pieces.append((stream, 0, 0, None, first, units))
        pieces += [(stream, 1, offset, None, first, units) for offset in OFFSETS]
        pieces += [(stream, 2, 0, before, first, units) for before in OFFSETS]
        pieces += [(stream, 2, offset, None, first, units) for offset in (1, -1)]
        cut = units - last
        pieces += [(stream, 2, 2, None, first, cut), (stream, 2, 2, None, first + cut, last)]
    return tuple(p for p in pieces if p[5])


def group_of(piece, slot):
    stream, phase, offset, before = piece[:4]
    if slot < 2:
        return (piece, slot)
    if phase == 0:
        return (piece, min(slot, 4))
    if phase == 1:
        return (stream, 1, slot // 2)
    if offset == 0 and before:
        return (stream, 2)
    if offset == 2:
        return (piece, slot // 2)
    return (piece, 2)


PIECES = cut_pieces()
GROUPS = {}
for _piece in PIECES:
    for _slot in range(6):
        GROUPS.setdefault(group_of(_piece, _slot), []).append((_piece, _slot))
ORDER = list(GROUPS)
CUTS = (5, 12, 20, 24, 24, 20, 14, 10)


def plan(hop=3.5, rate=46.5e3):
    needs = {}
    for piece in PIECES:
        stream, phase, offset, before = piece[:4]
        for part in range(2):
            if phase == 1 and offset:
                need = {(stream, 0, 0, offset, part)}
            elif phase == 2 and offset:
                need = {(stream, 1, by, offset, part) for by in OFFSETS}
            elif phase == 2 and before:
                need = {(stream, 0, 0, before, part)}
            else:
                need = set()
            needs[piece, part] = need
    free, heap, have, started = {}, [], set(), set()
    missing = {group: len(copies) for group, copies in GROUPS.items()}

    def send(piece, slot, now):
        stream, phase, _, before, _, units = piece
        link = (STREAMS[stream][2][phase], SLOTS[slot][0])
        size = units * 2048 * (4 if phase == 2 and before is None else 1)
        begin = max(now, free.get(link, 0.0))
        free[link] = begin + size / rate
        heapq.heappush(heap, (free[link] + hop, len(started), piece, slot))
        started.add((piece, slot))

    def ready(now):
        out = []
        for phase in range(3):
            for slot in range(4):
                for piece in PIECES:
                    if piece[1] == phase and (piece, slot) not in started:
                        if needs[piece, SLOTS[slot][2]] <= have:
                            send(piece, slot, now)
                            out.append((piece, slot))
        return out

    steps = [(None, ready(0.0))]
    while heap:
        now, _, piece, slot = heapq.heappop(heap)
        group = group_of(piece, slot)
        missing[group] -= 1
        if missing[group]:
            continue
        out = []
        for piece, slot in GROUPS[group]:
            way, whose, part = SLOTS[slot]
            if slot < 2:
                send(piece, slot + 4, now)
                out.append((piece, slot + 4))
            have.add((*piece[:3], {-1: -1, 1: 1, -2: 2, 2: 2}[whose - way], part))
        steps.append((group, out + ready(now)))
    return steps, now


def gather_kernel(x_ref, g, raw, source, landed, spread, load, a2a_send, a2a_recv, sent, got, passed, taken):
    row, y, zh = lax.axis_index("row"), lax.axis_index("col"), lax.axis_index("win")
    x, zl, core = row // 4, (row // 2) % 2, row % 2
    z = zh * 2 + zl
    here = {"x": x, "y": y, "z": z}

    def device(at, at_core):
        return (at["x"] * 4 + (at["z"] % 2) * 2 + at_core, at["y"], at["z"] // 2)

    def shifted(axis, by):
        return here | {axis: (here[axis] + by) % 4}

    me = core * 4 + y

    def member(by):
        m = (me + by) % 8
        return m, device(here | {"y": m % 4}, m // 4)

    fetch = pltpu.make_async_copy(x_ref, raw, load)
    fetch.start()
    barrier = pltpu.get_barrier_semaphore()

    def greet(other):
        pl.semaphore_signal(barrier, inc=1, device_id=other, device_id_type=MESH)

    def greet_member(by, carry):
        greet(member(by)[1])
        return carry

    def greet_neighbours(i, carry):
        greet(device(shifted("x", 1 + 2 * i), core))
        greet(device(shifted("z", 1 + 2 * i), core))
        return carry

    lax.fori_loop(1, 8, greet_member, 0)
    lax.fori_loop(0, 2, greet_neighbours, 0)
    fetch.wait()
    for m in range(8):
        values = [[raw[f, pl.ds(m * 32 + p, 16, stride=2), :] for p in range(2)] for f in range(2)]
        power = sum(v * v for pair in values for v in pair) / 2
        scale = jnp.maximum(jnp.sqrt(power), 1.0)
        for f in range(2):
            for p in range(2):
                source[m, f, p] = (values[f][p] / scale).astype(jnp.bfloat16)
    pl.semaphore_wait(barrier, 11)

    def swap(by):
        m, where = member(by)
        return pltpu.make_async_remote_copy(
            src_ref=source.at[m],
            dst_ref=landed.at[me],
            send_sem=a2a_send,
            recv_sem=a2a_recv,
            device_id=where,
            device_id_type=MESH,
        )

    for by in (2, 6, 1, 5, 3, 7, 4):
        swap(by).start()
    own = pltpu.make_async_copy(source.at[me], landed.at[me], load)
    own.start()
    own.wait()
    seven = landed.at[pl.ds(0, 7)]
    pltpu.make_async_copy(seven, seven, a2a_recv).wait()
    for f in range(2):
        for p in range(2):
            for s in range(8):
                spread[f, p, pl.ds(s * 16, 16), :] = landed[s, f, p].astype(jnp.float32)
    for f in range(2):
        for p in range(2):
            for b in range(16):
                windows = spread[f, p, pl.ds(b, 8, stride=16), :]
                g[core, y, b * 2 + f, p, x, z] = windows.astype(jnp.bfloat16)

    every = slice(None)

    def box(piece, by, part):
        stream, phase, offset, before, first, units = piece
        order = STREAMS[stream][2]
        at = dict(here)
        at[order[phase]] = (here[order[phase]] + by) % 4
        if phase:
            at[order[phase - 1]] = (here[order[phase - 1]] + offset) % 4
        if phase == 2:
            at[order[0]] = every if before is None else (here[order[0]] + before) % 4
        return g.at[core, at["y"], pl.ds(first, units), part, at["x"], at["z"]]

    def any_boxes(piece, count):
        first, units = piece[4:]
        ys, xs, zs, parts = next(
            dims
            for dims in itertools.product(range(1, 5), range(1, 5), range(1, 5), (1, 2))
            if math.prod(dims) == count
        )
        return g.at[core, pl.ds(0, ys), pl.ds(first, units), pl.ds(0, parts), pl.ds(0, xs), pl.ds(0, zs)]

    def launch(piece, slot):
        way, whose, part = SLOTS[slot]
        ref = box(piece, whose, part)
        pltpu.make_async_remote_copy(
            src_ref=ref,
            dst_ref=ref,
            send_sem=sent.at[piece[0], piece[1]],
            recv_sem=got.at[ORDER.index(group_of(piece, slot))],
            device_id=device(shifted(STREAMS[piece[0]][2][piece[1]], way), core),
            device_id_type=MESH,
        ).start()

    def hand_over(ref):
        pltpu.make_async_remote_copy(
            src_ref=ref,
            dst_ref=ref,
            send_sem=passed,
            recv_sem=taken,
            device_id=device(here, 1 - core),
            device_id_type=MESH,
        ).start()

    for group, copies in plan()[0]:
        refs = [g.at[core, y, :, :, x, z]]
        if group is not None:
            refs, count = [], 0
            for piece, slot in GROUPS[group]:
                way, whose, part = SLOTS[slot]
                refs.append(box(piece, whose - way, part))
                count += 4 if piece[1] == 2 and piece[3] is None else 1
            ref = refs[0] if len(refs) == 1 else any_boxes(GROUPS[group][0][0], count)
            pltpu.make_async_copy(ref, ref, got.at[ORDER.index(group)]).wait()
        for copy in copies:
            launch(*copy)
        for ref in refs:
            hand_over(ref)

    pltpu.make_async_copy(seven, seven, a2a_send).wait()
    for s, (first, units, _) in enumerate(STREAMS):
        for phase in range(3):
            xs = slice(0, 1) if phase == 0 else every
            zs = slice(0, 1) if phase < 2 else every
            ref = g.at[core, pl.ds(0, 3), pl.ds(first, units), :, xs, zs]
            pltpu.make_async_copy(ref, ref, sent.at[s, phase]).wait()
    pltpu.make_async_copy(g.at[core], g.at[core], passed).wait()
    pltpu.make_async_copy(g.at[1 - core], g.at[1 - core], taken).wait()


def gather(spectra):
    return pl.pallas_call(
        gather_kernel,
        out_shape=pltpu.VMEM(GATHERED, jnp.bfloat16),
        in_specs=[pl.BlockSpec(memory_space=pltpu.HBM)],
        out_specs=pl.BlockSpec(memory_space=pltpu.VMEM),
        scratch_shapes=[
            pltpu.VMEM((2, 256, BLOCK), jnp.float32),
            pltpu.VMEM((8, 2, 2, 16, BLOCK), jnp.bfloat16),
            pltpu.VMEM((8, 2, 2, 16, BLOCK), jnp.bfloat16),
            pltpu.VMEM((2, 2, BLOCK, BLOCK), jnp.float32),
            pltpu.SemaphoreType.DMA,
            pltpu.SemaphoreType.DMA,
            pltpu.SemaphoreType.DMA,
            pltpu.SemaphoreType.DMA((3, 3)),
            pltpu.SemaphoreType.DMA((len(ORDER),)),
            pltpu.SemaphoreType.DMA,
            pltpu.SemaphoreType.DMA,
        ],
        compiler_params=pltpu.CompilerParams(
            collective_id=0, has_side_effects=True, vmem_limit_bytes=32 << 20
        ),
    )(spectra)


def stack_kernel(rows_ref, cols_ref, g_ref, out_ref, held, sem):
    win = lax.axis_index("win")
    norm = 1.0 / jnp.sqrt(jnp.float32(BLOCK))
    for f in range(2):
        first = 0
        for tiles in CUTS if f == 0 else CUTS[::-1]:
            for k in range(first, first + tiles):
                turned = g_ref[rows_ref[k], f].T
                left = jnp.where(win == 0, turned[:64], turned[64:])
                crossed = jnp.concatenate([-left[:, 128:], left[:, :128]], axis=1)
                both = jnp.dot(
                    jnp.concatenate([left, crossed], axis=0),
                    g_ref[cols_ref[k], f],
                    preferred_element_type=jnp.float32,
                )
                both = both * norm
                held[f, k, 0] = both[:64]
                held[f, k, 1] = both[64:]
            put = pltpu.make_async_copy(
                held.at[f, pl.ds(first, tiles)], out_ref.at[pl.ds(first, tiles), f], sem
            )
            put.start()
            first += tiles
    pltpu.make_async_copy(held, held, sem).wait()


def stack_pairs(gathered, tile_rows, tile_cols):
    tiles = tile_rows.shape[0]
    return pl.pallas_call(
        stack_kernel,
        out_shape=jax.ShapeDtypeStruct((tiles, 2, 2, 64, BLOCK), jnp.float32),
        in_specs=[pl.BlockSpec(memory_space=pltpu.SMEM)] * 2 + [pl.BlockSpec(memory_space=pltpu.VMEM)],
        out_specs=pl.BlockSpec(memory_space=pl.ANY),
        scratch_shapes=[
            pltpu.VMEM((2, tiles, 2, 64, BLOCK), jnp.float32),
            pltpu.SemaphoreType.DMA,
        ],
        compiler_params=pltpu.CompilerParams(vmem_limit_bytes=24 << 20),
    )(tile_rows, tile_cols, gathered)


def on_device(spectra, tile_rows, tile_cols):
    values = spectra[0, :, 0].reshape(2, 2, BLOCK, BLOCK)
    values = jnp.transpose(values, (0, 2, 1, 3)).reshape(2, 2 * BLOCK, BLOCK)
    gathered = gather(pltpu.with_memory_space_constraint(values, pltpu.HBM))
    return stack_pairs(gathered.reshape(BLOCK, 2, 2 * BLOCK, BLOCK), tile_rows, tile_cols)


def solution(mesh):
    in_specs = (P("win", None, ("row", "col"), None, None), P(("row", "col")), P(("row", "col")))
    out_specs = P(("row", "col"), None, None, "win", None)
    return jax.shard_map(
        on_device, mesh=mesh, in_specs=in_specs, out_specs=out_specs, check_vma=False
    )
```

```python
import heapq
import itertools
import math

import jax
import jax.numpy as jnp
from jax import lax
from jax.experimental import pallas as pl
from jax.experimental.pallas import tpu as pltpu
from jax.sharding import PartitionSpec as P

MESH = pl.DeviceIdType.MESH
BLOCK = 128
GATHERED = (2, 4, 32, 2, 4, 4, 8, BLOCK)
STREAMS = ((0, 10, "xyz"), (10, 11, "yzx"), (21, 11, "zxy"))
OFFSETS = (0, 1, -1, 2)
SLOTS = ((1, 0, 0), (-1, 0, 1), (1, 0, 1), (-1, 0, 0), (1, -1, 0), (-1, 1, 1))


def cut_pieces(last=3):
    pieces = []
    for stream, (first, units, _) in enumerate(STREAMS):
        pieces.append((stream, 0, 0, None, first, units))
        pieces += [(stream, 1, offset, None, first, units) for offset in OFFSETS]
        pieces += [(stream, 2, 0, before, first, units) for before in OFFSETS]
        pieces += [(stream, 2, offset, None, first, units) for offset in (1, -1)]
        cut = units - last
        pieces += [(stream, 2, 2, None, first, cut), (stream, 2, 2, None, first + cut, last)]
    return tuple(p for p in pieces if p[5])


def group_of(piece, slot):
    stream, phase, offset, before = piece[:4]
    if slot < 2 or (phase == 2 and offset):
        return (piece, slot)
    if phase == 0:
        return (piece, min(slot, 4))
    if phase == 1:
        return (stream, 1, slot // 2)
    if offset == 0 and before:
        return (stream, 2)
    return (piece, 2)


PIECES = cut_pieces()
GROUPS = {}
for _piece in PIECES:
    for _slot in range(6):
        GROUPS.setdefault(group_of(_piece, _slot), []).append((_piece, _slot))
ORDER = list(GROUPS)
CUTS = (5, 12, 20, 24, 24, 20, 14, 10)


def plan(hop=3.5, rate=46.5e3):
    needs = {}
    for piece in PIECES:
        stream, phase, offset, before = piece[:4]
        for part in range(2):
            if phase == 1 and offset:
                need = {(stream, 0, 0, offset, part)}
            elif phase == 2 and offset:
                need = {(stream, 1, by, offset, part) for by in OFFSETS}
            elif phase == 2 and before:
                need = {(stream, 0, 0, before, part)}
            else:
                need = set()
            needs[piece, part] = need
    free, heap, have, started = {}, [], set(), set()
    missing = {group: len(copies) for group, copies in GROUPS.items()}

    def send(piece, slot, now):
        stream, phase, _, before, _, units = piece
        link = (STREAMS[stream][2][phase], SLOTS[slot][0])
        size = units * 2048 * (4 if phase == 2 and before is None else 1)
        begin = max(now, free.get(link, 0.0))
        free[link] = begin + size / rate
        heapq.heappush(heap, (free[link] + hop, len(started), piece, slot))
        started.add((piece, slot))

    def ready(now):
        out = []
        for phase in range(3):
            for slot in range(4):
                for piece in PIECES:
                    if piece[1] == phase and (piece, slot) not in started:
                        if needs[piece, SLOTS[slot][2]] <= have:
                            send(piece, slot, now)
                            out.append((piece, slot))
        return out

    steps = [(None, ready(0.0))]
    while heap:
        now, _, piece, slot = heapq.heappop(heap)
        group = group_of(piece, slot)
        missing[group] -= 1
        if missing[group]:
            continue
        out = []
        for piece, slot in GROUPS[group]:
            way, whose, part = SLOTS[slot]
            if slot < 2:
                send(piece, slot + 4, now)
                out.append((piece, slot + 4))
            have.add((*piece[:3], {-1: -1, 1: 1, -2: 2, 2: 2}[whose - way], part))
        steps.append((group, out + ready(now)))
    return steps, now


def gather_kernel(x_ref, g, raw, source, landed, spread, load, a2a_send, a2a_recv, sent, got, passed, taken):
    row, y, zh = lax.axis_index("row"), lax.axis_index("col"), lax.axis_index("win")
    x, zl, core = row // 4, (row // 2) % 2, row % 2
    z = zh * 2 + zl
    here = {"x": x, "y": y, "z": z}

    def device(at, at_core):
        return (at["x"] * 4 + (at["z"] % 2) * 2 + at_core, at["y"], at["z"] // 2)

    def shifted(axis, by):
        return here | {axis: (here[axis] + by) % 4}

    me = core * 4 + y

    def member(by):
        m = (me + by) % 8
        return m, device(here | {"y": m % 4}, m // 4)

    fetch = pltpu.make_async_copy(x_ref, raw, load)
    fetch.start()
    barrier = pltpu.get_barrier_semaphore()

    def greet(other):
        pl.semaphore_signal(barrier, inc=1, device_id=other, device_id_type=MESH)

    def greet_member(by, carry):
        greet(member(by)[1])
        return carry

    def greet_neighbours(i, carry):
        greet(device(shifted("x", 1 + 2 * i), core))
        greet(device(shifted("z", 1 + 2 * i), core))
        return carry

    lax.fori_loop(1, 8, greet_member, 0)
    lax.fori_loop(0, 2, greet_neighbours, 0)
    fetch.wait()
    for m in range(8):
        values = [[raw[f, pl.ds(m * 32 + p, 16, stride=2), :] for p in range(2)] for f in range(2)]
        power = sum(v * v for pair in values for v in pair) / 2
        scale = jnp.maximum(jnp.sqrt(power), 1.0)
        for f in range(2):
            for p in range(2):
                source[m, f, p] = (values[f][p] / scale).astype(jnp.bfloat16)
    pl.semaphore_wait(barrier, 11)

    def swap(by):
        m, where = member(by)
        return pltpu.make_async_remote_copy(
            src_ref=source.at[m],
            dst_ref=landed.at[me],
            send_sem=a2a_send,
            recv_sem=a2a_recv,
            device_id=where,
            device_id_type=MESH,
        )

    for by in (2, 6, 1, 5, 3, 7, 4):
        swap(by).start()
    own = pltpu.make_async_copy(source.at[me], landed.at[me], load)
    own.start()
    own.wait()
    seven = landed.at[pl.ds(0, 7)]
    pltpu.make_async_copy(seven, seven, a2a_recv).wait()
    for f in range(2):
        for p in range(2):
            for s in range(8):
                spread[f, p, pl.ds(s * 16, 16), :] = landed[s, f, p].astype(jnp.float32)
    for f in range(2):
        for p in range(2):
            for b in range(16):
                windows = spread[f, p, pl.ds(b, 8, stride=16), :]
                g[core, y, b * 2 + f, p, x, z] = windows.astype(jnp.bfloat16)

    every = slice(None)

    def box(piece, by, part):
        stream, phase, offset, before, first, units = piece
        order = STREAMS[stream][2]
        at = dict(here)
        at[order[phase]] = (here[order[phase]] + by) % 4
        if phase:
            at[order[phase - 1]] = (here[order[phase - 1]] + offset) % 4
        if phase == 2:
            at[order[0]] = every if before is None else (here[order[0]] + before) % 4
        return g.at[core, at["y"], pl.ds(first, units), part, at["x"], at["z"]]

    def any_boxes(piece, count):
        first, units = piece[4:]
        ys, xs, zs, parts = next(
            dims
            for dims in itertools.product(range(1, 5), range(1, 5), range(1, 5), (1, 2))
            if math.prod(dims) == count
        )
        return g.at[core, pl.ds(0, ys), pl.ds(first, units), pl.ds(0, parts), pl.ds(0, xs), pl.ds(0, zs)]

    def launch(piece, slot):
        way, whose, part = SLOTS[slot]
        ref = box(piece, whose, part)
        pltpu.make_async_remote_copy(
            src_ref=ref,
            dst_ref=ref,
            send_sem=sent.at[piece[0], piece[1]],
            recv_sem=got.at[ORDER.index(group_of(piece, slot))],
            device_id=device(shifted(STREAMS[piece[0]][2][piece[1]], way), core),
            device_id_type=MESH,
        ).start()

    def hand_over(ref):
        pltpu.make_async_remote_copy(
            src_ref=ref,
            dst_ref=ref,
            send_sem=passed,
            recv_sem=taken,
            device_id=device(here, 1 - core),
            device_id_type=MESH,
        ).start()

    for group, copies in plan()[0]:
        refs = [g.at[core, y, :, :, x, z]]
        if group is not None:
            refs, count = [], 0
            for piece, slot in GROUPS[group]:
                way, whose, part = SLOTS[slot]
                refs.append(box(piece, whose - way, part))
                count += 4 if piece[1] == 2 and piece[3] is None else 1
            ref = refs[0] if len(refs) == 1 else any_boxes(GROUPS[group][0][0], count)
            pltpu.make_async_copy(ref, ref, got.at[ORDER.index(group)]).wait()
        for copy in copies:
            launch(*copy)
        for ref in refs:
            hand_over(ref)

    pltpu.make_async_copy(seven, seven, a2a_send).wait()
    for s, (first, units, _) in enumerate(STREAMS):
        for phase in range(3):
            xs = slice(0, 1) if phase == 0 else every
            zs = slice(0, 1) if phase < 2 else every
            ref = g.at[core, pl.ds(0, 3), pl.ds(first, units), :, xs, zs]
            pltpu.make_async_copy(ref, ref, sent.at[s, phase]).wait()
    pltpu.make_async_copy(g.at[core], g.at[core], passed).wait()
    pltpu.make_async_copy(g.at[1 - core], g.at[1 - core], taken).wait()


def gather(spectra):
    return pl.pallas_call(
        gather_kernel,
        out_shape=pltpu.VMEM(GATHERED, jnp.bfloat16),
        in_specs=[pl.BlockSpec(memory_space=pltpu.HBM)],
        out_specs=pl.BlockSpec(memory_space=pltpu.VMEM),
        scratch_shapes=[
            pltpu.VMEM((2, 256, BLOCK), jnp.float32),
            pltpu.VMEM((8, 2, 2, 16, BLOCK), jnp.bfloat16),
            pltpu.VMEM((8, 2, 2, 16, BLOCK), jnp.bfloat16),
            pltpu.VMEM((2, 2, BLOCK, BLOCK), jnp.float32),
            pltpu.SemaphoreType.DMA,
            pltpu.SemaphoreType.DMA,
            pltpu.SemaphoreType.DMA,
            pltpu.SemaphoreType.DMA((3, 3)),
            pltpu.SemaphoreType.DMA((len(ORDER),)),
            pltpu.SemaphoreType.DMA,
            pltpu.SemaphoreType.DMA,
        ],
        compiler_params=pltpu.CompilerParams(
            collective_id=0, has_side_effects=True, vmem_limit_bytes=32 << 20
        ),
    )(spectra)


def stack_kernel(rows_ref, cols_ref, g_ref, out_ref, held, sem):
    win = lax.axis_index("win")
    norm = 1.0 / jnp.sqrt(jnp.float32(BLOCK))
    for f in range(2):
        first = 0
        for tiles in CUTS if f == 0 else CUTS[::-1]:
            for k in range(first, first + tiles):
                turned = g_ref[rows_ref[k], f].T
                left = jnp.where(win == 0, turned[:64], turned[64:])
                crossed = jnp.concatenate([-left[:, 128:], left[:, :128]], axis=1)
                both = jnp.dot(
                    jnp.concatenate([left, crossed], axis=0),
                    g_ref[cols_ref[k], f],
                    preferred_element_type=jnp.float32,
                )
                both = both * norm
                held[f, k, 0] = both[:64]
                held[f, k, 1] = both[64:]
            put = pltpu.make_async_copy(
                held.at[f, pl.ds(first, tiles)], out_ref.at[pl.ds(first, tiles), f], sem
            )
            put.start()
            first += tiles
    pltpu.make_async_copy(held, held, sem).wait()


def stack_pairs(gathered, tile_rows, tile_cols):
    tiles = tile_rows.shape[0]
    return pl.pallas_call(
        stack_kernel,
        out_shape=jax.ShapeDtypeStruct((tiles, 2, 2, 64, BLOCK), jnp.float32),
        in_specs=[pl.BlockSpec(memory_space=pltpu.SMEM)] * 2 + [pl.BlockSpec(memory_space=pltpu.VMEM)],
        out_specs=pl.BlockSpec(memory_space=pl.ANY),
        scratch_shapes=[
            pltpu.VMEM((2, tiles, 2, 64, BLOCK), jnp.float32),
            pltpu.SemaphoreType.DMA,
        ],
        compiler_params=pltpu.CompilerParams(vmem_limit_bytes=24 << 20),
    )(tile_rows, tile_cols, gathered)


def on_device(spectra, tile_rows, tile_cols):
    values = spectra[0, :, 0].reshape(2, 2, BLOCK, BLOCK)
    values = jnp.transpose(values, (0, 2, 1, 3)).reshape(2, 2 * BLOCK, BLOCK)
    gathered = gather(pltpu.with_memory_space_constraint(values, pltpu.HBM))
    return stack_pairs(gathered.reshape(BLOCK, 2, 2 * BLOCK, BLOCK), tile_rows, tile_cols)


def solution(mesh):
    in_specs = (P("win", None, ("row", "col"), None, None), P(("row", "col")), P(("row", "col")))
    out_specs = P(("row", "col"), None, None, "win", None)
    return jax.shard_map(
        on_device, mesh=mesh, in_specs=in_specs, out_specs=out_specs, check_vma=False
    )
```
